32 devices in a mesh: section: 2 (over y), ctx: 4 (over x, core), tensor: 4 (over z).
Axes of the slice: x: 2, y: 2, z: 4, core: 2. Of those that a mesh axis runs over, the one named last changes fastest.
Arguments:
- inputs: bfloat16 [2, 1024, 2048], P(None, 'ctx'), may hold values from -6 to 6
- cotangent: bfloat16 [2, 1024, 2048], P(None, 'ctx'), may hold values from -6 to 6
- query_weight: bfloat16 [2, 2048, 2048], P('section', 'ctx', 'tensor'), as said below
- key_weight: bfloat16 [2, 2048, 512], P('section', 'ctx', 'tensor'), as said below
- value_weight: bfloat16 [2, 2048, 512], P('section', 'ctx', 'tensor'), may hold values from -0.125 to 0.125
- output_weight: bfloat16 [2, 2048, 2048], P('section', 'tensor', 'ctx'), may hold values from -3 to 3
- gate_weight: bfloat16 [2, 2048, 8192], P('section', 'ctx', 'tensor'), may hold values from -0.125 to 0.125
- up_weight: bfloat16 [2, 2048, 8192], P('section', 'ctx', 'tensor'), may hold values from -0.125 to 0.125
- down_weight: bfloat16 [2, 8192, 2048], P('section', 'tensor', 'ctx'), may hold values from -0.0625 to 0.0625
- gain_attention: bfloat16 [2, 2048], P('section', 'ctx'), may hold values from 0.5 to 1.5
- gain_feedforward: bfloat16 [2, 2048], P('section', 'ctx'), may hold values from 0.5 to 1.5
Outputs:
- section_out: bfloat16 [2, 2, 1024, 2048], P('section', None, 'ctx')
- input_grads: bfloat16 [2, 2, 1024, 2048], P('section', None, 'ctx')
- query_grad: float32 [2, 2048, 2048], P('section', 'ctx', 'tensor')
- key_grad: float32 [2, 2048, 512], P('section', 'ctx', 'tensor')
- value_grad: float32 [2, 2048, 512], P('section', 'ctx', 'tensor')
- output_grad: float32 [2, 2048, 2048], P('section', 'tensor', 'ctx')
- gate_grad: float32 [2, 2048, 8192], P('section', 'ctx', 'tensor')
- up_grad: float32 [2, 2048, 8192], P('section', 'ctx', 'tensor')
- down_grad: float32 [2, 8192, 2048], P('section', 'tensor', 'ctx')
- gain_attention_grad: float32 [2, 2048], P('section', 'ctx')
- gain_feedforward_grad: float32 [2, 2048], P('section', 'ctx')
The draws below stay inside these ranges and needn't reach their ends.
Inputs may be any that keep to these rules, and one draw needn't show every extreme that they name: `query_weight`: entries lie within 100 / sqrt(2048) in magnitude. `key_weight`: entries lie within 4 / sqrt(2048) in magnitude.
All inputs are finite; a program needn't handle non-finite values.
Results may differ from the reference program's by a relative error of at most 0.025.
The reference program's roundings to bfloat16 on the way (of `attn_in`, `attended`, `ffn_in`, `hidden` and `grad_scores`) count: a program that leaves them out, or rounds other values in their place, can miss the bound.
Values may be sent and summed in bfloat16 or wider, within the bound.
No kernel may reach another device: no remote copies, remote signals or barrier semaphores. Data moves between devices by JAX's collectives and lax.ppermute only.
A program may use at most 320 MiB of HBM per device.

```python
import jax
import jax.numpy as jnp
from jax import lax

D = 2048
HEADS = 32
KV_HEADS = 8
HEAD_DIM = 64
FF = 8192
MICRO = 2
LAYERS = 2
SEQ = 1024


def paired_weights(key):
    query_seed = jax.random.fold_in(key, 101)
    key_seed = jax.random.fold_in(key, 102)
    key_part = jax.random.truncated_normal(key_seed, -4.0, 4.0, (LAYERS, D, KV_HEADS * HEAD_DIM), jnp.float32) * D ** (-0.5)
    query_part = jax.random.truncated_normal(query_seed, -4.0, 4.0, (LAYERS, D, HEADS * HEAD_DIM), jnp.float32) * D ** (-0.5)
    return (query_part, key_part)


def draw_query_weight(key, part):
    return paired_weights(key)[0].astype(jnp.bfloat16)


def draw_key_weight(key, part):
    return paired_weights(key)[1].astype(jnp.bfloat16)


def steps_of(own_key, dims, cuts, least, largest):
    def one(axis_at, parts):
        heights = jax.random.uniform(jax.random.fold_in(jax.random.fold_in(own_key, 6), axis_at), (parts,), jnp.float32, least / len(cuts), largest / len(cuts))
        return jnp.repeat(jnp.exp(heights), dims[axis_at] // parts).reshape((-1,) + (1,) * (len(dims) - axis_at - 1))

    factor_of = one(*cuts[0])
    for cut in cuts[1:]:
        factor_of = factor_of * one(*cut)
    return factor_of


def noise(rng, dims, deviation, bound, cuts=(), held_as=jnp.bfloat16):
    drawn = jax.random.normal(rng, dims, jnp.float32) * deviation
    if len(cuts) > 0:
        drawn = steps_of(rng, dims, cuts, -0.22, 0.18) * drawn
    return jnp.clip(drawn, min=-bound, max=bound).astype(held_as)


def setup_inputs(seed: int = 0) -> dict:
    key_of = jax.random.split(jax.random.key(seed), 12)
    inputs = noise(key_of[0], (MICRO, SEQ, D), 1.0, 6.0, ((1, 4),))
    cotangent = noise(key_of[1], (MICRO, SEQ, D), 1.0, 6.0, ((1, 4),))
    query_weight = draw_query_weight(jax.random.fold_in(key_of[11], 71), 0)
    key_weight = draw_key_weight(jax.random.fold_in(key_of[11], 71), 0)
    value_weight = noise(key_of[4], (LAYERS, D, KV_HEADS * HEAD_DIM), D ** -0.5, 0.125, ((0, 2), (1, 4), (2, 4)))
    output_weight = noise(key_of[5], (LAYERS, HEADS * HEAD_DIM, D), 4 ** -0.5, 3.0, ((0, 2), (1, 4), (2, 4)))
    gate_weight = noise(key_of[6], (LAYERS, D, FF), D ** -0.5, 0.125, ((0, 2), (1, 4), (2, 4)))
    up_weight = noise(key_of[7], (LAYERS, D, FF), D ** -0.5, 0.125, ((0, 2), (1, 4), (2, 4)))
    down_weight = noise(key_of[8], (LAYERS, FF, D), FF ** -0.5, 0.0625, ((0, 2), (1, 4), (2, 4)))
    gain_attention = jnp.clip(1.0 + 0.1 * jax.random.normal(key_of[9], (LAYERS, D), jnp.float32), 0.5, 1.5).astype(jnp.bfloat16)
    gain_feedforward = jnp.clip(1.0 + 0.1 * jax.random.normal(key_of[10], (LAYERS, D), jnp.float32), 0.5, 1.5).astype(jnp.bfloat16)
    return dict(inputs=inputs, cotangent=cotangent, query_weight=query_weight, key_weight=key_weight, value_weight=value_weight, output_weight=output_weight, gate_weight=gate_weight, up_weight=up_weight, down_weight=down_weight, gain_attention=gain_attention, gain_feedforward=gain_feedforward)


EPSILON = 1e-05
THETA_BASE = 500000.0
NEG_FILL = -1e+30

def rope_tables(positions):
    half_dim = HEAD_DIM // 2
    exponent = jnp.arange(half_dim, dtype=jnp.float32) * (-2.0 / HEAD_DIM)
    frequency = jnp.power(jnp.float32(THETA_BASE), exponent)
    angles = positions[:, None] * frequency[None, :]
    return (jnp.cos(angles), jnp.sin(angles))

def rotate(values, cosine, sine_table):
    row_count = values.shape[0]
    half_dim = cosine.shape[1]
    blocks = values.reshape(row_count, -1, 2 * half_dim)
    first_half = blocks[..., :half_dim]
    second_half = blocks[..., half_dim:]
    cos_rows = cosine[:, None, :]
    sin_rows = sine_table[:, None, :]
    turned = jnp.concatenate([first_half * cos_rows - second_half * sin_rows, second_half * cos_rows + first_half * sin_rows], axis=-1)
    return turned.reshape(row_count, -1)

def matmul(left, right):
    return jnp.dot(left, right, preferred_element_type=jnp.float32)

def norm_forward(values, gain_row):
    norm_scale = lax.rsqrt(lax.optimization_barrier(jnp.mean(values * values, axis=-1, keepdims=True)) + EPSILON)
    return (values * norm_scale * gain_row.astype(jnp.float32), norm_scale)

def norm_backward(grad_normed, values, norm_scale, gain_row):
    normed = values * norm_scale
    scaled = grad_normed * gain_row.astype(jnp.float32)
    grad_values = norm_scale * (scaled - normed * lax.optimization_barrier(jnp.mean(scaled * normed, axis=-1, keepdims=True)))
    gain_term = lax.optimization_barrier(jnp.sum(grad_normed * normed, axis=0))
    return (grad_values, gain_term)

def group_rows(matrix, group_size):
    row_count = matrix.shape[0]
    blocks = matrix.reshape(row_count, -1, group_size, HEAD_DIM)
    return blocks.transpose(1, 2, 0, 3).reshape(blocks.shape[1], group_size * row_count, HEAD_DIM)

def ungroup_rows(grouped, row_count):
    head_groups = grouped.shape[0]
    blocks = grouped.reshape(head_groups, -1, row_count, HEAD_DIM)
    return blocks.transpose(2, 0, 1, 3).reshape(row_count, -1)

def head_forward(query_rows, key_rows, value_rows, query_pos, key_pos):
    scores = matmul(query_rows, key_rows.T) * HEAD_DIM ** (-0.5)
    causal = key_pos[None, :] <= query_pos[:, None]
    masked = jnp.where(causal, scores, NEG_FILL)
    row_max = lax.optimization_barrier(jnp.max(masked, axis=-1))
    exp_weights = jnp.where(causal, jnp.exp(masked - row_max[:, None]), 0.0)
    row_total = lax.optimization_barrier(jnp.sum(exp_weights, axis=-1))
    mixed = matmul(exp_weights.astype(jnp.bfloat16), value_rows) / row_total[:, None]
    return (mixed, row_max + jnp.log(row_total))

def head_backward(query_rows, key_rows, value_rows, grad_rows, row_lse, row_delta, query_pos, key_pos):
    scores = matmul(query_rows, key_rows.T) * HEAD_DIM ** (-0.5)
    causal = key_pos[None, :] <= query_pos[:, None]
    soft_probs = jnp.where(causal, jnp.exp(scores - row_lse[:, None]), 0.0)
    grad_probs = matmul(grad_rows, value_rows.T)
    grad_scores = (soft_probs * (grad_probs - row_delta[:, None]) * HEAD_DIM ** (-0.5)).astype(jnp.bfloat16)
    grad_query = matmul(grad_scores, key_rows)
    grad_key = matmul(grad_scores.T, query_rows)
    grad_value = matmul(soft_probs.astype(jnp.bfloat16).T, grad_rows)
    return (grad_query, grad_key, grad_value)

def layer_forward(block_in, weights, cosine, sine_table, query_pos, key_pos):
    query_weight, key_weight, value_weight, output_weight, gate_weight, up_weight, down_weight, gain_attention, gain_feedforward = weights
    row_count = block_in.shape[0]
    group_size = HEADS // KV_HEADS
    values = block_in.astype(jnp.float32)
    normed, scale_attn = norm_forward(values, gain_attention)
    attn_in = normed.astype(jnp.bfloat16)
    query_rot = rotate(matmul(attn_in, query_weight), cosine, sine_table).astype(jnp.bfloat16)
    key_rot = rotate(matmul(attn_in, key_weight), cosine, sine_table).astype(jnp.bfloat16)
    value_rows = matmul(attn_in, value_weight).astype(jnp.bfloat16)
    grouped = group_rows(query_rot, group_size)
    key_heads = key_rot.reshape(row_count, -1, HEAD_DIM).transpose(1, 0, 2)
    value_heads = value_rows.reshape(row_count, -1, HEAD_DIM).transpose(1, 0, 2)
    mixed, row_lse = lax.map(lambda operand: head_forward(operand[0], operand[1], operand[2], query_pos, key_pos), (grouped, key_heads, value_heads))
    attended = ungroup_rows(mixed, row_count).astype(jnp.bfloat16)
    middle = values + matmul(attended, output_weight)
    normed_ffn, scale_ffn = norm_forward(middle, gain_feedforward)
    ffn_in = normed_ffn.astype(jnp.bfloat16)
    gate_act = matmul(ffn_in, gate_weight)
    up_act = matmul(ffn_in, up_weight)
    hidden = (jax.nn.silu(gate_act) * up_act).astype(jnp.bfloat16)
    block_out = middle + matmul(hidden, down_weight)
    saved = (block_in, scale_attn, attn_in, grouped, key_heads, value_heads, attended, row_lse, middle, scale_ffn, ffn_in, gate_act, up_act, hidden)
    return (block_out, saved)

def layer_backward(grad_out, saved, weights, cosine, sine_table, query_pos, key_pos):
    query_weight, key_weight, value_weight, output_weight, gate_weight, up_weight, down_weight, gain_attention, gain_feedforward = weights
    block_in, scale_attn, attn_in, grouped, key_heads, value_heads, attended, row_lse, middle, scale_ffn, ffn_in, gate_act, up_act, hidden = saved
    row_count = block_in.shape[0]
    group_size = HEADS // KV_HEADS
    grad_hidden = matmul(grad_out, down_weight.T)
    sigmoid = jax.nn.sigmoid(gate_act)
    grad_gate = (grad_hidden * up_act * sigmoid * (1.0 + gate_act * (1.0 - sigmoid))).astype(jnp.bfloat16)
    grad_up = (grad_hidden * gate_act * sigmoid).astype(jnp.bfloat16)
    grad_ffn_in = matmul(grad_gate, gate_weight.T) + matmul(grad_up, up_weight.T)
    grad_mid_norm, gain_ffn_term = norm_backward(grad_ffn_in, middle, scale_ffn, gain_feedforward)
    grad_middle = grad_out.astype(jnp.float32) + grad_mid_norm
    grad_mid_b = grad_middle.astype(jnp.bfloat16)
    grad_attended = matmul(grad_mid_b, output_weight.T).astype(jnp.bfloat16)
    grad_grouped = group_rows(grad_attended, group_size)
    att_grouped = group_rows(attended, group_size)
    row_delta = jnp.einsum('hqd,hqd->hq', grad_grouped.astype(jnp.float32), att_grouped.astype(jnp.float32))
    grad_query_g, grad_key_h, grad_value_h = lax.map(lambda operand: head_backward(operand[0], operand[1], operand[2], operand[3], operand[4], operand[5], query_pos, key_pos), (grouped, key_heads, value_heads, grad_grouped, row_lse, row_delta))
    grad_query = rotate(ungroup_rows(grad_query_g, row_count), cosine, -sine_table).astype(jnp.bfloat16)
    key_sum = grad_key_h.transpose(1, 0, 2).reshape(row_count, -1)
    value_sum = grad_value_h.transpose(1, 0, 2).reshape(row_count, -1)
    grad_key = rotate(key_sum, cosine, -sine_table).astype(jnp.bfloat16)
    grad_value = value_sum.astype(jnp.bfloat16)
    grad_attn_in = matmul(grad_query, query_weight.T) + matmul(grad_key, key_weight.T) + matmul(grad_value, value_weight.T)
    grad_in_norm, gain_attn_term = norm_backward(grad_attn_in, block_in.astype(jnp.float32), scale_attn, gain_attention)
    grad_in = grad_middle + grad_in_norm
    grad_terms = (matmul(attn_in.T, grad_query), matmul(attn_in.T, grad_key), matmul(attn_in.T, grad_value), matmul(attended.T, grad_mid_b), matmul(ffn_in.T, grad_gate), matmul(ffn_in.T, grad_up), matmul(hidden.T, grad_out), gain_attn_term, gain_ffn_term)
    return (grad_in, grad_terms)

def reference(inputs, cotangent, query_weight, key_weight, value_weight, output_weight, gate_weight, up_weight, down_weight, gain_attention, gain_feedforward):
    all_weights = (query_weight, key_weight, value_weight, output_weight, gate_weight, up_weight, down_weight, gain_attention, gain_feedforward)
    cosine, sine_table = rope_tables(jnp.arange(SEQ, dtype=jnp.float32))
    key_pos = jnp.arange(SEQ, dtype=jnp.int32)
    query_pos = jnp.tile(key_pos, HEADS // KV_HEADS)
    grad_sums = [jnp.zeros(member.shape, jnp.float32) for member in all_weights]
    outs_rows = [[None] * MICRO for layer_index in range(LAYERS)]
    grads_rows = [[None] * MICRO for layer_index in range(LAYERS)]
    for batch_index in range(MICRO):
        block = inputs[batch_index]
        saves = []
        for layer_index in range(LAYERS):
            layer_weights = tuple((member[layer_index] for member in all_weights))
            block_out, saved = layer_forward(block, layer_weights, cosine, sine_table, query_pos, key_pos)
            block = block_out.astype(jnp.bfloat16)
            outs_rows[layer_index][batch_index] = block
            saves.append(saved)
        grad_block = cotangent[batch_index]
        for layer_index in reversed(range(LAYERS)):
            layer_weights = tuple((member[layer_index] for member in all_weights))
            grad_in, grad_terms = layer_backward(grad_block, saves[layer_index], layer_weights, cosine, sine_table, query_pos, key_pos)
            grad_block = grad_in.astype(jnp.bfloat16)
            grads_rows[layer_index][batch_index] = grad_block
            for which in range(len(grad_sums)):
                grad_sums[which] = grad_sums[which].at[layer_index].add(grad_terms[which])
    section_out = jnp.stack([jnp.stack(row_list) for row_list in outs_rows])
    input_grads = jnp.stack([jnp.stack(row_list) for row_list in grads_rows])
    return (section_out, input_grads, grad_sums[0], grad_sums[1], grad_sums[2], grad_sums[3], grad_sums[4], grad_sums[5], grad_sums[6], grad_sums[7], grad_sums[8])
```

```python
import functools

import jax
import jax.numpy as jnp
from jax import lax
from jax.experimental import pallas as pl
from jax.experimental.pallas import tpu as pltpu
from jax.sharding import PartitionSpec as P

HEADS = 32
KV_HEADS = 8
HEAD_DIM = 64
GROUP = HEADS // KV_HEADS

EPSILON = 1e-05
THETA_BASE = 500000.0
NEG_FILL = -1e30
SCALE = HEAD_DIM ** (-0.5)


def dot_nn(left, right):
    return jnp.dot(left, right, preferred_element_type=jnp.float32)


def dot_nt(left, right):
    return lax.dot_general(left, right, (((1,), (1,)), ((), ())), preferred_element_type=jnp.float32)


def dot_tn(left, right):
    return lax.dot_general(left, right, (((0,), (0,)), ((), ())), preferred_element_type=jnp.float32)


def shifted(array, axis, by):
    count = lax.axis_size(axis)
    return lax.ppermute(array, axis, [(i, (i + by) % count) for i in range(count)])


def xored(array, axis, bit):
    count = lax.axis_size(axis)
    return lax.ppermute(array, axis, [(i, i ^ bit) for i in range(count)])


def reduce_rows(part):
    count = lax.axis_size("tensor")
    rows = part.shape[0] // count
    pieces = [part[k * rows : (k + 1) * rows] for k in range(count)]
    got = [shifted(pieces[k], "tensor", k) for k in range(1, count)]
    total = pieces[0].astype(jnp.float32)
    for piece in got:
        total = total + piece.astype(jnp.float32)
    return total


def gather_rows(own):
    count = lax.axis_size("tensor")
    return jnp.concatenate([own] + [shifted(own, "tensor", -k) for k in range(1, count)], axis=0)


def rotated_rows(array, index, count):
    rows = array.shape[0] // count
    return lax.dynamic_slice_in_dim(jnp.concatenate([array, array], axis=0), index * rows, array.shape[0], 0)


def natural_rows(array, index, count):
    rows = array.shape[0] // count
    start = ((count - index) % count) * rows
    return lax.dynamic_slice_in_dim(jnp.concatenate([array, array], axis=0), start, array.shape[0], 0)


def rope_tables(positions):
    half_dim = HEAD_DIM // 2
    exponent = jnp.arange(half_dim, dtype=jnp.float32) * (-2.0 / HEAD_DIM)
    frequency = jnp.power(jnp.float32(THETA_BASE), exponent)
    angles = positions[:, None] * frequency[None, :]
    return (jnp.cos(angles), jnp.sin(angles))


def turn(values, cosine, sine):
    width = values.shape[1]
    repeat = width // HEAD_DIM
    half = HEAD_DIM // 2
    up = jnp.concatenate([values[:, half:], values[:, :half]], axis=1)
    down = jnp.concatenate([values[:, -half:], values[:, :-half]], axis=1)
    lane = lax.broadcasted_iota(jnp.int32, values.shape, 1) % HEAD_DIM
    swapped = jnp.where(lane < half, up, down)
    return values * jnp.tile(cosine, (1, repeat)) + swapped * jnp.tile(sine, (1, repeat))


def attend_kernel(q_ref, kv_ref, qpos_ref, kpos_ref, out_ref, lse_ref):
    heads = q_ref.shape[1] // HEAD_DIM
    key_cols = kv_ref.shape[1] // 2
    causal = kpos_ref[...] <= qpos_ref[...]
    for head in range(heads):
        kv_head = head // GROUP
        cols = slice(head * HEAD_DIM, (head + 1) * HEAD_DIM)
        query = q_ref[:, cols]
        keys = kv_ref[:, kv_head * HEAD_DIM : (kv_head + 1) * HEAD_DIM]
        vals = kv_ref[:, key_cols + kv_head * HEAD_DIM : key_cols + (kv_head + 1) * HEAD_DIM]
        scores = jnp.where(causal, dot_nt(query, keys) * SCALE, NEG_FILL)
        row_max = jnp.max(scores, axis=1, keepdims=True)
        weights = jnp.where(causal, jnp.exp(scores - row_max), 0.0)
        total = jnp.sum(weights, axis=1, keepdims=True)
        mixed = dot_nn(weights.astype(jnp.bfloat16), vals) / total
        out_ref[:, cols] = mixed.astype(jnp.bfloat16)
        lse_ref[:, head : head + 1] = row_max + jnp.log(total)


def attend(query, kv_all, qpos, kpos):
    rows, width = query.shape
    return pl.pallas_call(
        attend_kernel,
        out_shape=(
            jax.ShapeDtypeStruct((rows, width), jnp.bfloat16),
            jax.ShapeDtypeStruct((rows, width // HEAD_DIM), jnp.float32),
        ),
        name="attend",
    )(query, kv_all, qpos, kpos)


def attend_back_kernel(
    q_ref, kv_ref, grad_ref, att_ref, lse_ref, qpos_ref, kpos_ref, dq_ref, dkv_ref
):
    heads = q_ref.shape[1] // HEAD_DIM
    key_cols = kv_ref.shape[1] // 2
    causal = kpos_ref[...] <= qpos_ref[...]
    for kv_head in range(heads // GROUP):
        kcols = slice(kv_head * HEAD_DIM, (kv_head + 1) * HEAD_DIM)
        vcols = slice(key_cols + kv_head * HEAD_DIM, key_cols + (kv_head + 1) * HEAD_DIM)
        keys = kv_ref[:, kcols]
        vals = kv_ref[:, vcols]
        key_sum = jnp.zeros(keys.shape, jnp.float32)
        val_sum = jnp.zeros(keys.shape, jnp.float32)
        for member in range(GROUP):
            head = kv_head * GROUP + member
            cols = slice(head * HEAD_DIM, (head + 1) * HEAD_DIM)
            query = q_ref[:, cols]
            grad = grad_ref[:, cols]
            delta = jnp.sum(
                grad.astype(jnp.float32) * att_ref[:, cols].astype(jnp.float32), axis=1, keepdims=True
            )
            scores = dot_nt(query, keys) * SCALE
            probs = jnp.where(causal, jnp.exp(scores - lse_ref[:, head : head + 1]), 0.0)
            grad_probs = dot_nt(grad, vals)
            grad_scores = (probs * (grad_probs - delta) * SCALE).astype(jnp.bfloat16)
            dq_ref[:, cols] = dot_nn(grad_scores, keys)
            key_sum = key_sum + dot_tn(grad_scores, query)
            val_sum = val_sum + dot_tn(probs.astype(jnp.bfloat16), grad)
        dkv_ref[:, kcols] = key_sum.astype(jnp.bfloat16)
        dkv_ref[:, vcols] = val_sum.astype(jnp.bfloat16)


def attend_back(query, kv_all, grad, attended, lse, qpos, kpos):
    return pl.pallas_call(
        attend_back_kernel,
        out_shape=(
            jax.ShapeDtypeStruct(query.shape, jnp.float32),
            jax.ShapeDtypeStruct(kv_all.shape, jnp.bfloat16),
        ),
        name="attend_back",
    )(query, kv_all, grad, attended, lse, qpos, kpos)


def norm_scale(values):
    return lax.rsqrt(jnp.mean(values * values, axis=-1, keepdims=True) + EPSILON)


def norm_backward(grad_normed, values, scale, gain_row):
    normed = values * scale
    scaled = grad_normed * gain_row
    grad_values = scale * (scaled - normed * jnp.mean(scaled * normed, axis=-1, keepdims=True))
    return (grad_values, jnp.sum(grad_normed * normed, axis=0))


def forward_layer(u, weights, tables):
    w_qkv, w_out, w_gate, w_up, w_down, gain_attn, gain_ffn = weights
    cosine, sine, qpos, kpos = tables
    own = u.shape[0] // lax.axis_size("tensor")
    values = u.astype(jnp.float32)
    attn_in = (values * norm_scale(values) * gain_attn).astype(jnp.bfloat16)
    qkv = dot_nn(attn_in, w_qkv)
    q_cols = w_qkv.shape[1] * HEADS // (HEADS + 2 * KV_HEADS)
    k_cols = q_cols // GROUP
    query = turn(qkv[:, :q_cols], cosine, sine).astype(jnp.bfloat16)
    keys = turn(qkv[:, q_cols : q_cols + k_cols], cosine, sine).astype(jnp.bfloat16)
    kv = jnp.concatenate([keys, qkv[:, q_cols + k_cols :].astype(jnp.bfloat16)], axis=1)
    kv_all = jnp.concatenate(
        [kv] + [shifted(kv, "ctx", k) for k in range(1, lax.axis_size("ctx"))], axis=0
    )
    attended, lse = attend(query, kv_all, qpos, kpos)
    middle = u[:own].astype(jnp.float32) + reduce_rows(dot_nn(attended, w_out).astype(jnp.bfloat16))
    scale_ffn = norm_scale(middle)
    ffn_in = gather_rows((middle * scale_ffn * gain_ffn).astype(jnp.bfloat16))
    gate_act = dot_nn(ffn_in, w_gate)
    up_act = dot_nn(ffn_in, w_up)
    hidden = (jax.nn.silu(gate_act) * up_act).astype(jnp.bfloat16)
    out_own = middle + reduce_rows(dot_nn(hidden, w_down).astype(jnp.bfloat16))
    out = gather_rows(out_own.astype(jnp.bfloat16))
    saved = (u[:own], attn_in, query, kv_all, attended, lse, middle, ffn_in, gate_act, up_act, hidden)
    return out, saved


def halved_sum(send, keep, axis):
    count = lax.axis_size("ctx")
    bit = 1
    while True:
        got = xored(send, "ctx", bit)
        total = keep.astype(jnp.float32) + got.astype(jnp.float32)
        bit *= 2
        if bit == count:
            return total
        total = total.astype(jnp.bfloat16)
        half = total.shape[axis] // 2
        keep = lax.slice_in_dim(total, 0, half, axis=axis)
        send = lax.slice_in_dim(total, half, 2 * half, axis=axis)


def backward_layer(grad_out, saved, weights, tables, xor_halves):
    w_qkv, w_out, w_gate, w_up, w_down, gain_attn, gain_ffn = weights
    cosine, sine, qpos, kpos = tables
    u_own, attn_in, query, kv_all, attended, lse, middle, ffn_in, gate_act, up_act, hidden = saved
    own, width = u_own.shape
    rows = attn_in.shape[0]
    sums = []
    grad_hidden = dot_nt(grad_out, w_down)
    sigmoid = jax.nn.sigmoid(gate_act)
    grad_gate = (grad_hidden * up_act * sigmoid * (1.0 + gate_act * (1.0 - sigmoid))).astype(jnp.bfloat16)
    grad_up = (grad_hidden * gate_act * sigmoid).astype(jnp.bfloat16)
    part = (dot_nt(grad_gate, w_gate) + dot_nt(grad_up, w_up)).astype(jnp.bfloat16)
    grad_ffn_in = reduce_rows(part)
    go_send, go_keep = xor_halves(grad_out)
    fi_send, fi_keep = xor_halves(ffn_in)

    def by_rows(pair, right):
        return halved_sum(
            dot_tn(pair[0], right).astype(jnp.bfloat16), dot_tn(pair[1], right).astype(jnp.bfloat16), 0
        )

    def by_cols(left, pair):
        return halved_sum(
            dot_tn(left, pair[0]).astype(jnp.bfloat16), dot_tn(left, pair[1]).astype(jnp.bfloat16), 1
        )

    sum_down = by_cols(hidden, (go_send, go_keep))
    sum_gate = by_rows((fi_send, fi_keep), grad_gate)
    sum_up = by_rows((fi_send, fi_keep), grad_up)
    grad_mid_norm, gain_ffn_term = norm_backward(grad_ffn_in, middle, norm_scale(middle), gain_ffn)
    grad_middle = grad_out[:own].astype(jnp.float32) + grad_mid_norm
    grad_mid_b = gather_rows(grad_middle.astype(jnp.bfloat16))
    grad_attended = dot_nt(grad_mid_b, w_out).astype(jnp.bfloat16)
    grad_query_rot, kv_terms = attend_back(query, kv_all, grad_attended, attended, lse, qpos, kpos)
    kv_sum = kv_terms[:rows].astype(jnp.float32)
    for k in range(1, lax.axis_size("ctx")):
        kv_sum = kv_sum + shifted(kv_terms[k * rows : (k + 1) * rows], "ctx", -k).astype(jnp.float32)
    k_cols = kv_sum.shape[1] // 2
    grad_qkv = jnp.concatenate(
        [
            turn(grad_query_rot, cosine, -sine).astype(jnp.bfloat16),
            turn(kv_sum[:, :k_cols], cosine, -sine).astype(jnp.bfloat16),
            kv_sum[:, k_cols:].astype(jnp.bfloat16),
        ],
        axis=1,
    )
    grad_attn_in = reduce_rows(dot_nt(grad_qkv, w_qkv).astype(jnp.bfloat16))
    sum_out = by_cols(attended, xor_halves(grad_mid_b))
    sum_qkv = by_rows(xor_halves(attn_in), grad_qkv)
    values = u_own.astype(jnp.float32)
    grad_in_norm, gain_attn_term = norm_backward(grad_attn_in, values, norm_scale(values), gain_attn)
    grad_in = gather_rows((grad_middle + grad_in_norm).astype(jnp.bfloat16))
    return grad_in, (sum_qkv, sum_out, sum_gate, sum_up, sum_down), (gain_attn_term, gain_ffn_term)


def on_device(
    inputs,
    cotangent,
    query_weight,
    key_weight,
    value_weight,
    output_weight,
    gate_weight,
    up_weight,
    down_weight,
    gain_attention,
    gain_feedforward,
):
    sections = lax.axis_size("section")
    section = lax.axis_index("section")
    tensors = lax.axis_size("tensor")
    tensor = lax.axis_index("tensor")
    ctxs = lax.axis_size("ctx")
    ctx = lax.axis_index("ctx")
    assert sections == 2 and inputs.shape[0] == sections
    assert ctxs & (ctxs - 1) == 0 and ctxs > 1
    is_first = section == 0
    rows, width = inputs.shape[1:]

    qkv_own = jnp.concatenate([query_weight[0], key_weight[0], value_weight[0]], axis=1)
    gains_own = jnp.concatenate([gain_attention, gain_feedforward], axis=0)
    layer_weights = [[None] * sections for unused in range(6)]
    own_shards = (qkv_own, output_weight[0], gate_weight[0], up_weight[0], down_weight[0], gains_own)
    axes = (0, 1, 0, 0, 1, 1)
    swapped = [lax.ppermute(shard, "section", [(0, 1), (1, 0)]) for shard in own_shards]
    for layer in range(sections):
        for which, (own_shard, other, axis) in enumerate(zip(own_shards, swapped, axes)):
            shard = jnp.where(section == layer, own_shard, other)
            layer_weights[which][layer] = lax.all_gather(shard, "ctx", axis=axis, tiled=True)

    offsets = rotated_rows(jnp.arange(rows, dtype=jnp.int32)[:, None], tensor, tensors)[:, 0]
    positions = ctx * rows + offsets
    key_positions = jnp.concatenate([((ctx - k) % ctxs) * rows + offsets for k in range(ctxs)])
    cosine_half, sine_half = rope_tables(positions.astype(jnp.float32))
    cosine = jnp.concatenate([cosine_half, cosine_half], axis=1)
    sine = jnp.concatenate([-sine_half, sine_half], axis=1)
    tables = (cosine, sine, positions[:, None], key_positions[None, :])

    bits = ctxs.bit_length() - 1
    order = [int(format(p, "0%db" % bits)[::-1], 2) for p in range(ctxs)]

    def xor_halves(matrix):
        blk = matrix.shape[1] // ctxs
        blocks = [
            lax.dynamic_slice_in_dim(matrix, (ctx ^ p) * blk, blk, 1) for p in order
        ]
        half = ctxs // 2
        return jnp.concatenate(blocks[half:], axis=1), jnp.concatenate(blocks[:half], axis=1)

    weights = []
    for layer in range(sections):
        gains = layer_weights[5][layer].astype(jnp.float32)
        weights.append(
            tuple(layer_weights[which][layer] for which in range(5)) + (gains[0:1], gains[1:2])
        )

    u = rotated_rows(lax.dynamic_index_in_dim(inputs, section, 0, keepdims=False), tensor, tensors)
    outs = []
    saves = []
    for layer in range(sections):
        u, saved = forward_layer(u, weights[layer], tables)
        outs.append(natural_rows(u, tensor, tensors))
        saves.append(saved)

    grad = rotated_rows(lax.dynamic_index_in_dim(cotangent, section, 0, keepdims=False), tensor, tensors)
    grads_in = [None] * sections
    sums = [None] * sections
    gain_terms = [None] * sections
    for layer in reversed(range(sections)):
        grad, sums[layer], gain_terms[layer] = backward_layer(
            grad, saves[layer], weights[layer], tables, xor_halves
        )
        grads_in[layer] = natural_rows(grad, tensor, tensors)

    def to_home(per_layer):
        got = [
            lax.ppermute(per_layer[layer], "section", [(1 - layer, layer)]) for layer in range(sections)
        ]
        return jnp.where(is_first, per_layer[0], per_layer[1]), jnp.where(is_first, got[0], got[1])

    def by_micro(per_layer):
        mine, other = to_home(per_layer)
        return jnp.where(is_first, jnp.stack([mine, other]), jnp.stack([other, mine]))

    def home_sum(which):
        per_layer = [sums[layer][which] for layer in range(sections)]
        got = [
            lax.ppermute(per_layer[layer].astype(jnp.bfloat16), "section", [(1 - layer, layer)])
            for layer in range(sections)
        ]
        full = [per_layer[layer] + got[layer].astype(jnp.float32) for layer in range(sections)]
        return jnp.where(is_first, full[0], full[1])

    section_out = by_micro(outs)
    input_grads = by_micro(grads_in)
    qkv_total = home_sum(0)
    q_cols = query_weight.shape[2]
    k_cols = key_weight.shape[2]
    gain_all = jnp.stack([term for layer in range(sections) for term in gain_terms[layer]])
    gain_all = lax.psum(gain_all, ("section", "ctx", "tensor"))
    gain_own = lax.dynamic_slice(
        gain_all, (2 * section, ctx * (width // ctxs)), (2, width // ctxs)
    )
    return (
        section_out[None],
        input_grads[None],
        qkv_total[None, :, :q_cols],
        qkv_total[None, :, q_cols : q_cols + k_cols],
        qkv_total[None, :, q_cols + k_cols :],
        home_sum(1)[None],
        home_sum(2)[None],
        home_sum(3)[None],
        home_sum(4)[None],
        gain_own[0:1],
        gain_own[1:2],
    )


def solution(mesh):
    in_specs = (
        P(None, "ctx", None),
        P(None, "ctx", None),
        P("section", "ctx", "tensor"),
        P("section", "ctx", "tensor"),
        P("section", "ctx", "tensor"),
        P("section", "tensor", "ctx"),
        P("section", "ctx", "tensor"),
        P("section", "ctx", "tensor"),
        P("section", "tensor", "ctx"),
        P("section", "ctx"),
        P("section", "ctx"),
    )
    out_specs = (
        P("section", None, "ctx", None),
        P("section", None, "ctx", None),
        P("section", "ctx", "tensor"),
        P("section", "ctx", "tensor"),
        P("section", "ctx", "tensor"),
        P("section", "tensor", "ctx"),
        P("section", "ctx", "tensor"),
        P("section", "ctx", "tensor"),
        P("section", "tensor", "ctx"),
        P("section", "ctx"),
        P("section", "ctx"),
    )
    return jax.shard_map(
        on_device, mesh=mesh, in_specs=in_specs, out_specs=out_specs, check_vma=False
    )
```
